1024 devices in a mesh: blk: 128 (over y, z), sub: 8 (over x, core).
Axes of the slice: x: 4, y: 8, z: 16, core: 2. Of those that a mesh axis runs over, the one named last changes fastest.
Arguments:
- east_flow: float32 [2048, 12, 7168], P(('blk', 'sub')), may hold values from -6 to 6
- north_flow: float32 [2048, 12, 7168], P(('blk', 'sub')), may hold values from -6 to 6
- levels: int32 [2048, 7168], P(('blk', 'sub')), may hold values from 0 to 12
- coriolis: float32 [2048], P(('blk', 'sub')), may hold values from -1 to 1
- thickness: float32 [12], replicated, may hold values from 0.02 to 0.12
- surface: float32 [2048, 7168], P('blk', 'sub'), may hold values from -6 to 6
Outputs:
- east_next: float32 [2048, 12, 7168], P(('blk', 'sub'))
- north_next: float32 [2048, 12, 7168], P(('blk', 'sub'))
- surface_next: float32 [2048, 7168], P('blk', 'sub')
The draws below stay inside these ranges and needn't reach their ends.
Inputs may be any that keep to these rules, and one draw needn't show every extreme that they name: levels[j,i] active levels of the column counted from the top, 0 on land, up to 12.
All inputs are finite; a program needn't handle non-finite values.
Results may differ from the reference program's by a relative error of at most 0.00002.
Values sent between devices are 32-bit elements; how exact they have to be, the bound alone decides.
A program may use at most 64 MiB of HBM per device.

```python
import math
import jax
import jax.numpy as jnp
from jax import lax

NLON = 7168
K = 12
NSUB = 4
NLAT = 2048


def place_ends(drawn, own_key, low, high):
    longest = drawn.shape.index(max(drawn.shape))
    spots = []
    for shift in (0, 1):
        where = [jax.random.randint(jax.random.fold_in(own_key, axis), (), 0, length) for axis, length in enumerate(drawn.shape)]
        where[longest] = (where[longest] + shift) % drawn.shape[longest]
        spots.append(tuple(where))
    return drawn.at[spots[0]].set(low).at[spots[1]].set(high)


def steps_of(stream_key, dims, cuts, low, largest):
    def one(axis_at, blocks):
        steps = jax.random.uniform(jax.random.fold_in(jax.random.fold_in(stream_key, 6), axis_at), (blocks,), jnp.float32, low / len(cuts), largest / len(cuts))
        return jnp.repeat(jnp.exp(steps), dims[axis_at] // blocks).reshape((-1,) + (1,) * (len(dims) - axis_at - 1))

    factor_of = one(*cuts[0])
    for cut in cuts[1:]:
        factor_of = factor_of * one(*cut)
    return factor_of


def scatter_about(rng, dims, deviation, most, cuts=(), held_as=jnp.bfloat16):
    loudness = steps_of(rng, dims, cuts, -0.22, 0.18) if cuts else 1.0
    drawn = jax.random.normal(rng, dims, jnp.float32) * deviation * loudness
    return jnp.minimum(jnp.maximum(drawn, -most), most).astype(held_as)


def setup_inputs(seed: int = 0) -> dict:
    key_list = jax.random.split(jax.random.key(seed), 7)
    east_flow = scatter_about(key_list[0], (NLAT, K, NLON), 1.0, 6.0, ((0, 1024),), jnp.float32)
    north_flow = scatter_about(key_list[1], (NLAT, K, NLON), 1.0, 6.0, ((0, 1024),), jnp.float32)
    levels = place_ends(jax.random.randint(key_list[2], (NLAT, NLON), 0, K + 1), jax.random.fold_in(key_list[2], 1), 0, K).astype(jnp.int32)
    coriolis = jnp.clip(jax.random.uniform(key_list[3], (NLAT,), jnp.float32, -1.0, 1.0) * steps_of(key_list[3], (NLAT,), ((0, 1024),), -0.4, 0.0), -1.0, 1.0)
    thickness = jnp.clip(jnp.exp(jax.random.uniform(key_list[4], (K,), jnp.float32, math.log(0.02), math.log(0.12))), 0.02, 0.12)
    surface = scatter_about(key_list[5], (NLAT, NLON), 1.0, 6.0, ((0, 128), (1, 8)), jnp.float32)
    return {"east_flow": east_flow, "north_flow": north_flow, "levels": levels, "coriolis": coriolis, "thickness": thickness, "surface": surface}


second_weights = (-1.0 / 12.0, 16.0 / 12.0, -30.0 / 12.0, 16.0 / 12.0, -1.0 / 12.0)
first_weights = (1.0 / 12.0, -8.0 / 12.0, 0.0, 8.0 / 12.0, -1.0 / 12.0)
viscosity = 0.05
mixing = 0.1
rotation = 0.2
continuity = 0.5
pressure = 0.5


def stencil(padded, along, weights):
    length = padded.shape[along] - 4
    total = None
    for offset in range(5):
        if weights[offset] != 0.0:
            term = weights[offset] * lax.slice_in_dim(padded, offset, offset + length, axis=along)
            total = term if total is None else total + term
    return total


def periodic(field, weights):
    total = None
    for offset in range(5):
        if weights[offset] != 0.0:
            term = weights[offset] * jnp.roll(field, 2 - offset, axis=-1)
            total = term if total is None else total + term
    return total


def vertical(field, along):
    count = field.shape[along]
    upper = lax.slice_in_dim(field, 0, 1, axis=along)
    lower = lax.slice_in_dim(field, count - 1, count, axis=along)
    padded = jnp.concatenate((upper, field, lower), axis=along)
    return lax.slice_in_dim(padded, 2, count + 2, axis=along) - 2.0 * field + lax.slice_in_dim(padded, 0, count, axis=along)


def pad_rows(field):
    widths = [(2, 2)] + [(0, 0)] * (field.ndim - 1)
    return jnp.pad(field, widths)


def reference(east_flow, north_flow, levels, coriolis, thickness, surface):
    depth_ids = lax.broadcasted_iota(jnp.int32, east_flow.shape, 1)
    wet = (depth_ids < levels[:, None, :]).astype(jnp.float32)
    east = east_flow * wet
    north = north_flow * wet
    rotor = coriolis[:, None, None]

    def provisional(field, other, factor):
        laplace = stencil(pad_rows(field), 0, second_weights) + periodic(field, second_weights)
        return wet * (field + viscosity * laplace + mixing * vertical(field, 1) + factor * rotation * rotor * other)

    east_star = provisional(east, north, 1.0)
    north_star = provisional(north, east, -1.0)
    layer = thickness[None, :, None]
    east_sum = jnp.sum(layer * east_star, axis=1)
    north_sum = jnp.sum(layer * north_star, axis=1)
    depth = jnp.sum(layer * wet, axis=1)
    east_tr = east_sum
    north_tr = north_sum
    height = surface
    for substep in range(NSUB):
        height = height - continuity * (periodic(east_tr, first_weights) + stencil(pad_rows(north_tr), 0, first_weights))
        east_tr = east_tr - pressure * depth * periodic(height, first_weights)
        north_tr = north_tr - pressure * depth * stencil(pad_rows(height), 0, first_weights)
    inverse = jnp.where(levels > 0, 1.0 / jnp.where(levels > 0, depth, 1.0), 0.0)
    east_next = east_star + wet * ((east_tr - east_sum) * inverse)[:, None, :]
    north_next = north_star + wet * ((north_tr - north_sum) * inverse)[:, None, :]
    return east_next, north_next, height
```

```python
import functools

import jax
import jax.numpy as jnp
from jax import lax
from jax.experimental import pallas as pl
from jax.experimental.pallas import tpu as pltpu
from jax.sharding import PartitionSpec as P

MESH = pl.DeviceIdType.MESH
T = 128
NSUB = 4
viscosity = 0.05
mixing = 0.1
rotation = 0.2
continuity = 0.5
pressure = 0.5


def up8(n):
    return (n + 7) // 8 * 8


def tiles_of(value):
    return [value[:, t * T : (t + 1) * T] for t in range(value.shape[1] // T)]


def shift_lanes(x, by):
    return pltpu.roll(x, by % x.shape[1], 1)


def shift_rows(x, by):
    return pltpu.roll(x, by % x.shape[0], 0)


def ring_extended(x):
    w = x.shape[1]
    return jnp.concatenate([shift_rows(x[:, w - T :], 1), x, shift_rows(x[:, :T], -1)], axis=1)


def dx12(q):
    return shift_lanes(q, 2) - shift_lanes(q, -2) + 8.0 * (shift_lanes(q, -1) - shift_lanes(q, 1))


def dy12(q0, q1):
    u0, u1 = shift_rows(q0, -1), shift_rows(q1, -1)
    d0, d1 = shift_rows(q0, 1), shift_rows(q1, 1)
    return d0 - u0 + 8.0 * (q1 - d1), d1 - u1 + 8.0 * (u0 - q0)


def kernel(
    NB, NS, K, NL,
    thick, cor, e_hbm, n_hbm, l_hbm, h_hbm,
    eo_hbm, no_hbm, so_hbm,
    ein, nin, lin, hin, lev, M, RP, RN, ST, fs, fr, ds_, dr, B, G, cs, cr, X, inv, eo, no, so,
    in_sem, h_sem, bulk_sem, a2a_sem, z_sem, x_sem, out_sem,
):
    W = NL // NS
    TT = W // T
    L = W + 2 * T
    QF, QD, QC = up8((TT + 2) * 4), up8((TT + 2) * 2), up8(TT * 4)
    PK = 2 * NL // T
    b = lax.axis_index("blk")
    s = lax.axis_index("sub")
    flat = b * NS + s
    total = NB * NS
    prev = lax.rem(flat + total - 1, total)
    nxt = lax.rem(flat + 1, total)
    prev = (lax.div(prev, NS), lax.rem(prev, NS))
    nxt = (lax.div(nxt, NS), lax.rem(nxt, NS))
    zup = (lax.rem(b + 1, NB), s)
    zdn = (lax.rem(b + NB - 1, NB), s)
    peers = [(b, lax.rem(s + j, NS)) for j in range(1, NS)]

    loads = [
        pltpu.make_async_copy(l_hbm, lin, in_sem.at[0]),
        pltpu.make_async_copy(e_hbm, ein, in_sem.at[1]),
        pltpu.make_async_copy(n_hbm, nin, in_sem.at[2]),
    ]
    h_loads = [
        pltpu.make_async_copy(
            h_hbm.at[:, pl.ds(t * T, T)], hin.at[pl.ds(t * 16, 16), :], h_sem.at[t]
        )
        for t in range(TT)
    ]
    for c in loads + h_loads:
        c.start()
    barrier = pltpu.get_barrier_semaphore()
    for peer in [prev, nxt, zup, zdn] + peers:
        pl.semaphore_signal(barrier, inc=1, device_id=peer, device_id_type=MESH)

    loads[0].wait()
    levs = []
    for r in range(2):
        v = jnp.concatenate([lin[pl.ds(t * 2 + r, 8, stride=2 * TT), :] for t in range(TT)], axis=1)
        lev[r] = v
        levs.append(v)
    for r in range(2):
        acc = jnp.zeros((8, W), jnp.float32)
        for k in range(K):
            acc = acc + jnp.where(levs[r] > k, thick[k], 0.0)
        inv[r] = jnp.where(levs[r] > 0, 1.0 / jnp.where(levs[r] > 0, acc, 1.0), 0.0)
        ext = ring_extended(acc)
        for t, v in enumerate(tiles_of(ext)):
            ds_[pl.ds(t * 2 + r, 8, stride=QD), :] = v
    for c in h_loads:
        c.wait()
    for r in range(2):
        for t in range(TT):
            G[0, r, 8:16, (t + 1) * T : (t + 2) * T] = hin[pl.ds(t * 16 + r, 8, stride=2), :]
    loads[1].wait()
    loads[2].wait()

    def mask_level(k, _):
        for r in range(2):
            wet = lev[r] > k
            for f, src in ((0, ein), (1, nin)):
                v = jnp.concatenate(
                    [src[pl.ds(k * PK + t * 2 + r, 8, stride=2 * TT), :] for t in range(TT)], axis=1
                )
                M[k, f, r] = jnp.where(wet, v, 0.0)
        return 0

    lax.fori_loop(0, K, mask_level, 0)

    pl.semaphore_wait(barrier, 4 + NS - 1)

    def a2a(src, dst, q, which):
        out = []
        for j in range(1, NS):
            to = lax.rem(s + j, NS)
            out.append(
                pltpu.make_async_remote_copy(
                    src_ref=src.at[pl.ds(pl.multiple_of(to * q, 8), q), :],
                    dst_ref=dst.at[pl.ds(pl.multiple_of(s * q, 8), q), :],
                    send_sem=a2a_sem.at[which, 0, j - 1],
                    recv_sem=a2a_sem.at[which, 1, j - 1],
                    device_id=(b, to),
                    device_id_type=MESH,
                )
            )
        return out

    def own(src, dst, q):
        at = pl.ds(pl.multiple_of(s * q, 8), q)
        dst[at, :] = src[at, :]

    d_copies = a2a(ds_, dr, QD, 0)
    for c in d_copies:
        c.start()
    right, left = (b, lax.rem(s + 1, NS)), (b, lax.rem(s + NS - 1, NS))
    h_copies = [
        pltpu.make_async_remote_copy(
            src_ref=G.at[0, :, pl.ds(8, 8), pl.ds(at, T)],
            dst_ref=G.at[0, :, pl.ds(8, 8), pl.ds(to, T)],
            send_sem=x_sem.at[0, i],
            recv_sem=x_sem.at[1, i],
            device_id=peer,
            device_id_type=MESH,
        )
        for i, (at, to, peer) in enumerate(((W, 0, right), (T, W + T, left)))
    ]
    for c in h_copies:
        c.start()

    def bulk(k, way):
        return pltpu.make_async_remote_copy(
            src_ref=M.at[k],
            dst_ref=(RN if way == 0 else RP).at[k],
            send_sem=bulk_sem.at[way, 0, k],
            recv_sem=bulk_sem.at[way, 1, k],
            device_id=prev if way == 0 else nxt,
            device_id_type=MESH,
        )

    def start_bulk(k, _):
        bulk(k, 0).start()
        bulk(k, 1).start()
        return 0

    lax.fori_loop(0, K, start_bulk, 0)
    own(ds_, dr, QD)

    cv = viscosity / 12.0

    def local_level(k, _):
        above = jnp.maximum(k - 1, 0)
        below = jnp.minimum(k + 1, K - 1)
        for r in range(2):
            turn = rotation * cor[r]
            for f in range(2):
                x = M[k, f, r]
                ext = ring_extended(x)
                near = (shift_lanes(ext, 1) + shift_lanes(ext, -1))[:, T : T + W] + M[k, f, 1 - r]
                far = (shift_lanes(ext, 2) + shift_lanes(ext, -2))[:, T : T + W]
                lap = 16.0 * near - far
                vz = M[above, f, r] + M[below, f, r]
                other = M[k, 1 - f, r]
                sign = turn if f == 0 else -turn
                ST[k, f, r] = (1.0 - 60.0 * cv - 2.0 * mixing) * x + cv * lap + mixing * vz + sign * other
        return 0

    lax.fori_loop(0, K, local_level, 0)

    for c in d_copies:
        c.wait_recv()
    for c in h_copies:
        c.wait_recv()
    for r in range(2):
        for t in range(TT + 2):
            G[1, r, 8:16, t * T : (t + 1) * T] = dr[pl.ds(t * 2 + r, 8, stride=QD), :]

    def zcopies(buf, which):
        return [
            pltpu.make_async_remote_copy(
                src_ref=buf.at[:, :, pl.ds(8, 8), :],
                dst_ref=buf.at[:, :, pl.ds(to, 8), :],
                send_sem=z_sem.at[which, 0, i],
                recv_sem=z_sem.at[which, 1, i],
                device_id=peer,
                device_id_type=MESH,
            )
            for i, (to, peer) in enumerate(((0, zup), (16, zdn)))
        ]

    g_copies = zcopies(G, 0)
    for c in g_copies:
        c.start()

    gp = jnp.where(flat > 0, cv, 0.0)
    gn = jnp.where(flat < total - 1, cv, 0.0)

    def finish_level(k, sums):
        bulk(k, 0).wait_recv()
        bulk(k, 1).wait_recv()
        th = thick[k]
        out = []
        for f in range(2):
            p0, p1 = RP[k, f, 0], RP[k, f, 1]
            n0, n1 = RN[k, f, 0], RN[k, f, 1]
            for r in range(2):
                if r == 0:
                    add = gp * (16.0 * p1 - p0) - gn * n0
                else:
                    add = gn * (16.0 * n0 - n1) - gp * p1
                v = jnp.where(lev[r] > k, ST[k, f, r] + add, 0.0)
                ST[k, f, r] = v
                out.append(sums[2 * f + r] + th * v)
        return tuple(out)

    sums = lax.fori_loop(0, K, finish_level, tuple(jnp.zeros((8, W), jnp.float32) for _ in range(4)))
    for f in range(2):
        for r in range(2):
            for t, v in enumerate(tiles_of(ring_extended(sums[2 * f + r]))):
                fs[pl.ds(t * 4 + f * 2 + r, 8, stride=QF), :] = v
    f_copies = a2a(fs, fr, QF, 1)
    for c in f_copies:
        c.start()
    own(fs, fr, QF)
    for c in f_copies:
        c.wait_recv()
    for f in range(2):
        for r in range(2):
            for t in range(TT + 2):
                B[f, r, 8:16, t * T : (t + 1) * T] = fr[pl.ds(t * 4 + f * 2 + r, 8, stride=QF), :]
    b_copies = zcopies(B, 1)
    for c in b_copies:
        c.start()
    for c in g_copies:
        c.wait_recv()
    for c in b_copies:
        c.wait_recv()

    row = lax.broadcasted_iota(jnp.int32, (24, T), 0)
    inside = jnp.logical_and(
        jnp.logical_or(row >= 8, b > 0), jnp.logical_or(row < 16, b < NB - 1)
    )
    inside = jnp.concatenate([inside.astype(jnp.float32)] * (TT + 2), axis=1)
    east = [B[0, r] for r in range(2)]
    north = [jnp.where(inside > 0.0, B[1, r], 0.0) for r in range(2)]
    high = [jnp.where(inside > 0.0, G[0, r], 0.0) for r in range(2)]
    deep = [jnp.where(inside > 0.0, G[1, r], 0.0) * (pressure / 12.0) for r in range(2)]
    step = inside * (continuity / 12.0)
    for _ in range(NSUB):
        dn = dy12(north[0], north[1])
        high = [high[r] - step * (dx12(east[r]) + dn[r]) for r in range(2)]
        dh = dy12(high[0], high[1])
        east = [east[r] - deep[r] * dx12(high[r]) for r in range(2)]
        north = [north[r] - deep[r] * dh[r] for r in range(2)]
    for f, field in ((0, east), (1, north)):
        for r in range(2):
            change = field[r][8:16, T : T + W] - B[f, r, 8:16, T : T + W]
            for t, v in enumerate(tiles_of(change)):
                cs[pl.ds(t * 4 + f * 2 + r, 8, stride=QC), :] = v
    c_copies = a2a(cs, cr, QC, 2)
    for c in c_copies:
        c.start()
    for r in range(2):
        for t in range(TT):
            so[pl.ds(t * 16 + r, 8, stride=2), :] = high[r][8:16, (t + 1) * T : (t + 2) * T]
    so_copies = [
        pltpu.make_async_copy(
            so.at[pl.ds(t * 16, 16), :], so_hbm.at[:, pl.ds(t * T, T)], h_sem.at[t]
        )
        for t in range(TT)
    ]
    for c in so_copies:
        c.start()
    own(cs, cr, QC)
    for c in c_copies:
        c.wait_recv()
    for f in range(2):
        for r in range(2):
            v = jnp.concatenate(
                [cr[pl.ds(t * 4 + f * 2 + r, 8, stride=QC), :] for t in range(TT)], axis=1
            )
            X[f, r] = v * inv[r]

    def store_level(k, _):
        for r in range(2):
            wet = lev[r] > k
            for f, dst in ((0, eo), (1, no)):
                v = ST[k, f, r] + jnp.where(wet, X[f, r], 0.0)
                for t in range(TT):
                    dst[pl.ds(k * PK + t * 2 + r, 8, stride=2 * TT), :] = v[:, t * T : (t + 1) * T]
        return 0

    lax.fori_loop(0, K, store_level, 0)
    outs = [
        pltpu.make_async_copy(eo, eo_hbm, out_sem.at[0]),
        pltpu.make_async_copy(no, no_hbm, out_sem.at[1]),
    ]
    for c in outs:
        c.start()

    def drain(k, _):
        bulk(k, 0).wait_send()
        bulk(k, 1).wait_send()
        return 0

    lax.fori_loop(0, K, drain, 0)
    for c in d_copies + h_copies + f_copies + g_copies + b_copies + c_copies:
        c.wait_send()
    for c in outs + so_copies:
        c.wait()


def flattened(x):
    k = x.shape[1]
    x = x.reshape(2, k, -1, T).transpose(1, 2, 0, 3)
    return x.reshape(-1, T)


def unflattened(x, k):
    x = x.reshape(k, -1, 2, T).transpose(2, 0, 1, 3)
    return x.reshape(2, k, -1)


def body(NB, NS, east_flow, north_flow, levels, coriolis, thickness, surface):
    _, K, NL = east_flow.shape
    W = NL // NS
    TT = W // T
    L = W + 2 * T
    rows = K * 2 * NL // T
    QF, QD, QC = up8((TT + 2) * 4), up8((TT + 2) * 2), up8(TT * 4)
    f32 = jnp.float32
    lev = levels.reshape(2, -1, T).transpose(1, 0, 2).reshape(-1, T)
    any_ = pl.BlockSpec(memory_space=pl.ANY)
    smem = pl.BlockSpec(memory_space=pltpu.SMEM)
    big = pltpu.VMEM((K, 2, 2, 8, W), f32)
    dma = pltpu.SemaphoreType.DMA
    eo, no, so = pl.pallas_call(
        functools.partial(kernel, NB, NS, K, NL),
        out_shape=(
            jax.ShapeDtypeStruct((rows, T), f32),
            jax.ShapeDtypeStruct((rows, T), f32),
            jax.ShapeDtypeStruct((16, W), f32),
        ),
        in_specs=[smem, smem, any_, any_, any_, any_],
        out_specs=[any_, any_, any_],
        scratch_shapes=[
            pltpu.VMEM((rows, T), f32),
            pltpu.VMEM((rows, T), f32),
            pltpu.VMEM((2 * NL // T, T), jnp.int32),
            pltpu.VMEM((16 * TT, T), f32),
            pltpu.VMEM((2, 8, W), jnp.int32),
            big,
            big,
            big,
            big,
            pltpu.VMEM((NS * QF, T), f32),
            pltpu.VMEM((NS * QF, T), f32),
            pltpu.VMEM((NS * QD, T), f32),
            pltpu.VMEM((NS * QD, T), f32),
            pltpu.VMEM((2, 2, 24, L), f32),
            pltpu.VMEM((2, 2, 24, L), f32),
            pltpu.VMEM((NS * QC, T), f32),
            pltpu.VMEM((NS * QC, T), f32),
            pltpu.VMEM((2, 2, 8, W), f32),
            pltpu.VMEM((2, 8, W), f32),
            pltpu.VMEM((rows, T), f32),
            pltpu.VMEM((rows, T), f32),
            pltpu.VMEM((16 * TT, T), f32),
            dma((3,)),
            dma((TT,)),
            dma((2, 2, K)),
            dma((3, 2, NS - 1)),
            dma((2, 2, 2)),
            dma((2, 2)),
            dma((2,)),
        ],
        compiler_params=pltpu.CompilerParams(collective_id=0, has_side_effects=True),
    )(thickness, coriolis, flattened(east_flow), flattened(north_flow), lev, surface)
    return unflattened(eo, K), unflattened(no, K), so


def solution(mesh):
    NB, NS = mesh.shape["blk"], mesh.shape["sub"]
    both = ("blk", "sub")
    return jax.shard_map(
        functools.partial(body, NB, NS),
        mesh=mesh,
        in_specs=(P(both, None, None), P(both, None, None), P(both, None), P(both), P(), P("blk", "sub")),
        out_specs=(P(both, None, None), P(both, None, None), P("blk", "sub")),
        check_vma=False,
    )
```

```python
import functools

import jax
import jax.numpy as jnp
from jax import lax
from jax.experimental import pallas as pl
from jax.experimental.pallas import tpu as pltpu
from jax.sharding import PartitionSpec as P

MESH = pl.DeviceIdType.MESH
T = 128
NSUB = 4
VMEM_LIMIT = 16 << 20
B1, B2, B3 = 3, 6, 10
F2 = 4
FAR_FIRST = (4, 3, 5, 2, 6, 1, 7)
viscosity = 0.05
mixing = 0.1
rotation = 0.2
continuity = 0.5
pressure = 0.5


def up8(n):
    return (n + 7) // 8 * 8


def tiles_of(value):
    return [value[:, t * T : (t + 1) * T] for t in range(value.shape[1] // T)]


def shift_lanes(x, by):
    return pltpu.roll(x, by % x.shape[1], 1)


def shift_rows(x, by):
    return pltpu.roll(x, by % x.shape[0], 0)


def ring_extended(x):
    w = x.shape[1]
    return with_rim(x, shift_rows(x[:, w - T :], 1), shift_rows(x[:, :T], -1))


def with_rim(x, before, after):
    low = lax.broadcasted_iota(jnp.int32, before.shape, 1) < T // 2
    return jnp.concatenate([x, jnp.where(low, after, before)], axis=1)


def dx12(q):
    return shift_lanes(q, 2) - shift_lanes(q, -2) + 8.0 * (shift_lanes(q, -1) - shift_lanes(q, 1))


def dy12(q0, q1):
    u0, u1 = shift_rows(q0, -1), shift_rows(q1, -1)
    d0, d1 = shift_rows(q0, 1), shift_rows(q1, 1)
    return d0 - u0 + 8.0 * (q1 - d1), d1 - u1 + 8.0 * (u0 - q0)


def kernel(
    NB, NS, K, NL,
    t_hbm, c_hbm, e_hbm, n_hbm, l_hbm, h_hbm,
    eo, no, so,
    thick, cor, ein, nin, lin, hin, lev, M, RP, RN, ST, fs, fr, ds_, dr, B, G, HX, cs, cr, X, inv,
    LP, LN, levx, PP, PN, QP, QN,
    in_sem, h_sem, bulk_sem, a2a_sem, z_sem, x_sem, n_sem,
):
    W = NL // NS
    TT = W // T
    L = W + T
    QF, QD, QC = up8((TT + 1) * 4), up8((TT + 1) * 2), up8(TT * 4)
    PK = 2 * NL // T
    b = lax.axis_index("blk")
    s = lax.axis_index("sub")
    flat = b * NS + s
    total = NB * NS
    prev = lax.rem(flat + total - 1, total)
    nxt = lax.rem(flat + 1, total)
    prev = (lax.div(prev, NS), lax.rem(prev, NS))
    nxt = (lax.div(nxt, NS), lax.rem(nxt, NS))
    zup = (lax.rem(b + 1, NB), s)
    zdn = (lax.rem(b + NB - 1, NB), s)
    peers = [(b, lax.rem(s + j, NS)) for j in range(1, NS)]
    has_prev, has_next = flat > 0, flat < total - 1
    has_dn, has_up = b > 0, b < NB - 1
    one = lambda there: jnp.where(there, 1, 0)

    loads = [
        pltpu.make_async_copy(l_hbm, lin, in_sem.at[0]),
        pltpu.make_async_copy(e_hbm, ein, in_sem.at[1]),
        pltpu.make_async_copy(n_hbm, nin, in_sem.at[2]),
        pltpu.make_async_copy(t_hbm, thick, in_sem.at[3]),
        pltpu.make_async_copy(c_hbm, cor, in_sem.at[4]),
    ]
    h_loads = [
        pltpu.make_async_copy(
            h_hbm.at[:, pl.ds(t * T, T)], hin.at[pl.ds(t * 16, 16), :], h_sem.at[t]
        )
        for t in range(TT)
    ]
    for c in loads + h_loads:
        c.start()
    barrier = pltpu.get_barrier_semaphore()
    for peer in peers:
        pl.semaphore_signal(barrier, inc=1, device_id=peer, device_id_type=MESH)
    for there, peer in ((has_prev, prev), (has_next, nxt), (has_dn, zdn), (has_up, zup)):

        @pl.when(there)
        def _():
            pl.semaphore_signal(barrier, inc=1, device_id=peer, device_id_type=MESH)


    def clear(there, refs):
        @pl.when(jnp.logical_not(there))
        def _():
            for ref in refs:
                ref[...] = jnp.zeros(ref.shape, ref.dtype)

    clear(has_prev, [QP, LP])
    clear(has_next, [QN, LN])
    clear(has_dn, [ref.at[i, j, pl.ds(0, 8)] for ref in (B, G) for i in range(2) for j in range(2)])
    clear(has_up, [ref.at[i, j, pl.ds(16, 8)] for ref in (B, G) for i in range(2) for j in range(2)])
    for there, buf in ((has_prev, RP), (has_next, RN)):

        @pl.when(jnp.logical_not(there))
        def _():
            def zero_level(k, _):
                for f in range(2):
                    for r in range(2):
                        buf[k, f, r] = jnp.zeros((8, W), jnp.float32)
                return 0

            lax.fori_loop(0, K, zero_level, 0)

    pl.semaphore_wait(barrier, NS - 1 + one(has_prev) + one(has_next) + one(has_dn) + one(has_up))

    def to_neighbours(src_up, src_down, dst_from_prev, dst_from_next, which):
        return [
            (
                out,
                back,
                pltpu.make_async_remote_copy(
                    src_ref=src,
                    dst_ref=dst,
                    send_sem=n_sem.at[which, 0, i],
                    recv_sem=n_sem.at[which, 1, i],
                    device_id=peer,
                    device_id_type=MESH,
                ),
            )
            for i, (src, dst, peer, out, back) in enumerate(
                (
                    (src_up, dst_from_prev, nxt, has_next, has_prev),
                    (src_down, dst_from_next, prev, has_prev, has_next),
                )
            )
        ]

    def start_if(copies):
        for out, _, c in copies:
            pl.when(out)(c.start)

    def wait_recv_if(copies):
        for _, back, c in copies:
            pl.when(back)(c.wait_recv)

    def wait_send_if(copies):
        for out, _, c in copies:
            pl.when(out)(c.wait_send)

    l_copies = to_neighbours(l_hbm, l_hbm, LP, LN, 0)
    start_if(l_copies)

    def a2a(src, dst, q, which):
        out = []
        for j in FAR_FIRST:
            to = lax.rem(s + j, NS)
            out.append(
                pltpu.make_async_remote_copy(
                    src_ref=src.at[pl.ds(pl.multiple_of(to * q, 8), q), :],
                    dst_ref=dst.at[pl.ds(pl.multiple_of(s * q, 8), q), :],
                    send_sem=a2a_sem.at[which, 0, j - 1],
                    recv_sem=a2a_sem.at[which, 1, j - 1],
                    device_id=(b, to),
                    device_id_type=MESH,
                )
            )
        return out

    def own(src, dst, q):
        at = pl.ds(pl.multiple_of(s * q, 8), q)
        dst[at, :] = src[at, :]

    loads[0].wait()
    loads[3].wait()
    loads[4].wait()
    levs = []
    for r in range(2):
        v = jnp.concatenate([lin[pl.ds(t * 2 + r, 8, stride=2 * TT), :] for t in range(TT)], axis=1)
        lev[r] = v
        levs.append(v)
    for r in range(2):
        acc = jnp.zeros((8, W), jnp.float32)
        for k in range(K):
            acc = acc + jnp.where(levs[r] > k, thick[k], 0.0)
        inv[r] = jnp.where(levs[r] > 0, 1.0 / jnp.where(levs[r] > 0, acc, 1.0), 0.0)
        ext = ring_extended(acc)
        for t, v in enumerate(tiles_of(ext)):
            ds_[pl.ds(t * 2 + r, 8, stride=QD), :] = v
    for c in h_loads:
        c.wait()
    for r in range(2):
        for t in range(TT):
            G[0, r, 8:16, t * T : (t + 1) * T] = hin[pl.ds(t * 16 + r, 8, stride=2), :]
    d_copies = a2a(ds_, dr, QD, 0)
    for c in d_copies:
        c.start()
    right, left = (b, lax.rem(s + 1, NS)), (b, lax.rem(s + NS - 1, NS))
    h_copies = [
        pltpu.make_async_remote_copy(
            src_ref=G.at[0, :, pl.ds(8, 8), pl.ds(at, T)],
            dst_ref=HX.at[i],
            send_sem=x_sem.at[0, i],
            recv_sem=x_sem.at[1, i],
            device_id=peer,
            device_id_type=MESH,
        )
        for i, (at, peer) in enumerate(((W - T, right), (0, left)))
    ]
    for c in h_copies:
        c.start()
    loads[1].wait()
    loads[2].wait()

    def mask_level(k, _):
        for r in range(2):
            wet = lev[r] > k
            for f, src in ((0, ein), (1, nin)):
                v = jnp.concatenate(
                    [src[pl.ds(k * PK + t * 2 + r, 8, stride=2 * TT), :] for t in range(TT)], axis=1
                )
                M[k, f, r] = jnp.where(wet, v, 0.0)
        return 0

    lax.fori_loop(0, K, mask_level, 0)

    def bulk(k, way):
        return pltpu.make_async_remote_copy(
            src_ref=M.at[k],
            dst_ref=(RN if way == 0 else RP).at[k],
            send_sem=bulk_sem.at[way, 0, k],
            recv_sem=bulk_sem.at[way, 1, k],
            device_id=prev if way == 0 else nxt,
            device_id_type=MESH,
        )

    def start_bulk(first, last):
        for k in range(first, last):
            pl.when(has_prev)(bulk(k, 0).start)
            pl.when(has_next)(bulk(k, 1).start)

    start_bulk(0, B1)
    own(ds_, dr, QD)

    cv = viscosity / 12.0

    def local_level(k, sums):
        above = jnp.maximum(k - 1, 0)
        below = jnp.minimum(k + 1, K - 1)
        th = thick[k]
        out = []
        for f in range(2):
            for r in range(2):
                turn = rotation * cor[r]
                x = M[k, f, r]
                ext = ring_extended(x)
                near = (shift_lanes(ext, 1) + shift_lanes(ext, -1))[:, :W] + M[k, f, 1 - r]
                far = (shift_lanes(ext, 2) + shift_lanes(ext, -2))[:, :W]
                lap = 16.0 * near - far
                vz = M[above, f, r] + M[below, f, r]
                other = M[k, 1 - f, r]
                sign = turn if f == 0 else -turn
                v = (1.0 - 60.0 * cv - 2.0 * mixing) * x + cv * lap + mixing * vz + sign * other
                ST[k, f, r] = v
                out.append(sums[2 * f + r] + jnp.where(lev[r] > k, th * v, 0.0))
        return tuple(out)

    zeros = tuple(jnp.zeros((8, W), jnp.float32) for _ in range(4))
    sums = lax.fori_loop(0, K // 2, local_level, zeros)

    wait_recv_if(l_copies)
    for i, src in ((0, LP), (1, LN)):
        for r in range(2):
            levx[i, r] = jnp.concatenate(
                [src[pl.ds(t * 2 + r, 8, stride=2 * TT), :] for t in range(TT)], axis=1
            )

    def partial_level(i):
        def level(k, sums):
            th = thick[k]
            wet = [levx[i, r] > k for r in range(2)]
            out = []
            for f in range(2):
                m0, m1 = M[k, f, 0], M[k, f, 1]
                terms = (-m0, 16.0 * m0 - m1) if i == 0 else (16.0 * m1 - m0, -m1)
                for r in range(2):
                    out.append(sums[2 * f + r] + jnp.where(wet[r], th * terms[r], 0.0))
            return tuple(out)

        return level

    for i, dst in ((0, PP), (1, PN)):
        part = lax.fori_loop(0, K, partial_level(i), zeros)
        for f in range(2):
            for r in range(2):
                dst[f, r] = part[2 * f + r]
    p_copies = to_neighbours(PN, PP, QP, QN, 1)
    start_if(p_copies)
    start_bulk(B1, B2)
    sums = lax.fori_loop(K // 2, K, local_level, sums)

    for c in d_copies + h_copies:
        c.wait_recv()
    for r in range(2):
        G[0, r, 8:16, W:L] = with_rim(HX[1, r], HX[0, r], HX[1, r])[:, T:]
        for t in range(TT + 1):
            G[1, r, 8:16, t * T : (t + 1) * T] = dr[pl.ds(t * 2 + r, 8, stride=QD), :]

    def zcopies(buf, which):
        return [
            (
                out,
                back,
                pltpu.make_async_remote_copy(
                    src_ref=buf.at[:, :, pl.ds(8, 8), :],
                    dst_ref=buf.at[:, :, pl.ds(to, 8), :],
                    send_sem=z_sem.at[which, 0, i],
                    recv_sem=z_sem.at[which, 1, i],
                    device_id=peer,
                    device_id_type=MESH,
                ),
            )
            for i, (to, peer, out, back) in enumerate(((0, zup, has_up, has_dn), (16, zdn, has_dn, has_up)))
        ]

    g_copies = zcopies(G, 0)
    start_if(g_copies)

    wait_recv_if(p_copies)
    for f in range(2):
        for r in range(2):
            v = sums[2 * f + r] + cv * QP[f, r] + cv * QN[f, r]
            for t, v in enumerate(tiles_of(ring_extended(v))):
                fs[pl.ds(t * 4 + f * 2 + r, 8, stride=QF), :] = v
    f_copies = a2a(fs, fr, QF, 1)
    for c in f_copies:
        c.start()
    own(fs, fr, QF)

    def finish_level(k, _):
        pl.when(has_next)(bulk(k, 0).wait_recv)
        pl.when(has_prev)(bulk(k, 1).wait_recv)
        for f in range(2):
            p0, p1 = RP[k, f, 0], RP[k, f, 1]
            n0, n1 = RN[k, f, 0], RN[k, f, 1]
            for r in range(2):
                if r == 0:
                    add = cv * (16.0 * p1 - p0) - cv * n0
                else:
                    add = cv * (16.0 * n0 - n1) - cv * p1
                ST[k, f, r] = ST[k, f, r] + add
        return 0

    for c in f_copies:
        c.wait_recv()
    for f in range(2):
        for r in range(2):
            for t in range(TT + 1):
                B[f, r, 8:16, t * T : (t + 1) * T] = fr[pl.ds(t * 4 + f * 2 + r, 8, stride=QF), :]
    b_copies = zcopies(B, 1)
    start_if(b_copies)
    start_bulk(B2, B3)
    lax.fori_loop(0, F2, finish_level, 0)
    wait_recv_if(g_copies)
    wait_recv_if(b_copies)

    row = lax.broadcasted_iota(jnp.int32, (24, T), 0)
    inside = jnp.logical_and(jnp.logical_or(row >= 8, has_dn), jnp.logical_or(row < 16, has_up))
    step = jnp.concatenate([jnp.where(inside, continuity / 12.0, 0.0)] * (TT + 1), axis=1)
    east = [B[0, r] for r in range(2)]
    north = [B[1, r] for r in range(2)]
    high = [G[0, r] for r in range(2)]
    deep = [G[1, r] * (pressure / 12.0) for r in range(2)]
    for _ in range(NSUB):
        dn = dy12(north[0], north[1])
        high = [high[r] - step * (dx12(east[r]) + dn[r]) for r in range(2)]
        dh = dy12(high[0], high[1])
        east = [east[r] - deep[r] * dx12(high[r]) for r in range(2)]
        north = [north[r] - deep[r] * dh[r] for r in range(2)]
    for f, field in ((0, east), (1, north)):
        for r in range(2):
            change = field[r][8:16, :W] - B[f, r, 8:16, :W]
            for t, v in enumerate(tiles_of(change)):
                cs[pl.ds(t * 4 + f * 2 + r, 8, stride=QC), :] = v
    c_copies = a2a(cs, cr, QC, 2)
    for c in c_copies:
        c.start()
    start_bulk(B3, K)
    for r in range(2):
        for t in range(TT):
            so[pl.ds(t * 16 + r, 8, stride=2), :] = high[r][8:16, t * T : (t + 1) * T]
    own(cs, cr, QC)
    lax.fori_loop(F2, K, finish_level, 0)
    for c in c_copies:
        c.wait_recv()
    for f in range(2):
        for r in range(2):
            v = jnp.concatenate(
                [cr[pl.ds(t * 4 + f * 2 + r, 8, stride=QC), :] for t in range(TT)], axis=1
            )
            X[f, r] = v * inv[r]

    def store_level(k, _):
        for r in range(2):
            wet = lev[r] > k
            for f, dst in ((0, eo), (1, no)):
                v = jnp.where(wet, ST[k, f, r] + X[f, r], 0.0)
                for t in range(TT):
                    dst[pl.ds(k * PK + t * 2 + r, 8, stride=2 * TT), :] = v[:, t * T : (t + 1) * T]
        return 0

    lax.fori_loop(0, K, store_level, 0)

    def drain(k, _):
        pl.when(has_prev)(bulk(k, 0).wait_send)
        pl.when(has_next)(bulk(k, 1).wait_send)
        return 0

    lax.fori_loop(0, K, drain, 0)
    for c in d_copies + h_copies + f_copies + c_copies:
        c.wait_send()
    for c in (l_copies, p_copies, g_copies, b_copies):
        wait_send_if(c)


def store_kernel(e, n, h, eo, no, ho, sem, h_sem):
    TT = ho.shape[1] // T
    copies = [pltpu.make_async_copy(e, eo, sem.at[0]), pltpu.make_async_copy(n, no, sem.at[1])]
    copies += [
        pltpu.make_async_copy(h.at[pl.ds(t * 16, 16), :], ho.at[:, pl.ds(t * T, T)], h_sem.at[t])
        for t in range(TT)
    ]
    for c in copies:
        c.start()
    for c in copies:
        c.wait()


def flattened(x):
    k = x.shape[1]
    x = x.reshape(2, k, -1, T).transpose(1, 2, 0, 3)
    return x.reshape(-1, T)


def unflattened(x, k):
    x = x.reshape(k, -1, 2, T).transpose(2, 0, 1, 3)
    return x.reshape(2, k, -1)


def body(NB, NS, east_flow, north_flow, levels, coriolis, thickness, surface):
    _, K, NL = east_flow.shape
    W = NL // NS
    TT = W // T
    L = W + T
    rows = K * 2 * NL // T
    QF, QD, QC = up8((TT + 1) * 4), up8((TT + 1) * 2), up8(TT * 4)
    f32 = jnp.float32
    lev = levels.reshape(2, -1, T).transpose(1, 0, 2).reshape(-1, T)
    any_ = pl.BlockSpec(memory_space=pl.ANY)
    hbm = pl.BlockSpec(memory_space=pltpu.HBM)
    vmem = pl.BlockSpec(memory_space=pltpu.VMEM)
    big = pltpu.VMEM((K, 2, 2, 8, W), f32)
    sums = pltpu.VMEM((2, 2, 8, W), f32)
    dma = pltpu.SemaphoreType.DMA
    eo, no, so = pl.pallas_call(
        functools.partial(kernel, NB, NS, K, NL),
        out_shape=(
            jax.ShapeDtypeStruct((rows, T), f32),
            jax.ShapeDtypeStruct((rows, T), f32),
            jax.ShapeDtypeStruct((16 * TT, T), f32),
        ),
        in_specs=[hbm] * 6,
        out_specs=[vmem] * 3,
        scratch_shapes=[
            pltpu.SMEM((K,), f32),
            pltpu.SMEM((2,), f32),
            pltpu.VMEM((rows, T), f32),
            pltpu.VMEM((rows, T), f32),
            pltpu.VMEM((2 * NL // T, T), jnp.int32),
            pltpu.VMEM((16 * TT, T), f32),
            pltpu.VMEM((2, 8, W), jnp.int32),
            big,
            big,
            big,
            big,
            pltpu.VMEM((NS * QF, T), f32),
            pltpu.VMEM((NS * QF, T), f32),
            pltpu.VMEM((NS * QD, T), f32),
            pltpu.VMEM((NS * QD, T), f32),
            pltpu.VMEM((2, 2, 24, L), f32),
            pltpu.VMEM((2, 2, 24, L), f32),
            pltpu.VMEM((2, 2, 8, T), f32),
            pltpu.VMEM((NS * QC, T), f32),
            pltpu.VMEM((NS * QC, T), f32),
            sums,
            pltpu.VMEM((2, 8, W), f32),
            pltpu.VMEM((2 * NL // T, T), jnp.int32),
            pltpu.VMEM((2 * NL // T, T), jnp.int32),
            pltpu.VMEM((2, 2, 8, W), jnp.int32),
            sums,
            sums,
            sums,
            sums,
            dma((5,)),
            dma((TT,)),
            dma((2, 2, K)),
            dma((3, 2, NS - 1)),
            dma((2, 2, 2)),
            dma((2, 2)),
            dma((2, 2, 2)),
        ],
        compiler_params=pltpu.CompilerParams(
            collective_id=0, has_side_effects=True, vmem_limit_bytes=VMEM_LIMIT
        ),
    )(*[pltpu.with_memory_space_constraint(x, pltpu.HBM) for x in (thickness, coriolis, flattened(east_flow), flattened(north_flow), lev, surface)])
    eo, no, so = pl.pallas_call(
        store_kernel,
        out_shape=(
            jax.ShapeDtypeStruct((rows, T), f32),
            jax.ShapeDtypeStruct((rows, T), f32),
            jax.ShapeDtypeStruct((16, W), f32),
        ),
        in_specs=[any_] * 3,
        out_specs=[hbm] * 3,
        scratch_shapes=[dma((2,)), dma((TT,))],
        compiler_params=pltpu.CompilerParams(vmem_limit_bytes=VMEM_LIMIT),
    )(eo, no, so)
    return unflattened(eo, K), unflattened(no, K), so


def solution(mesh):
    NB, NS = mesh.shape["blk"], mesh.shape["sub"]
    both = ("blk", "sub")
    return jax.shard_map(
        functools.partial(body, NB, NS),
        mesh=mesh,
        in_specs=(P(both, None, None), P(both, None, None), P(both, None), P(both), P(), P("blk", "sub")),
        out_specs=(P(both, None, None), P(both, None, None), P("blk", "sub")),
        check_vma=False,
    )
```

```python
import functools

import jax
import jax.numpy as jnp
from jax import lax
from jax.experimental import pallas as pl
from jax.experimental.pallas import tpu as pltpu
from jax.sharding import PartitionSpec as P

MESH = pl.DeviceIdType.MESH
T = 128
NSUB = 4
VMEM_LIMIT = 16 << 20
INNER = (0, 3, 6, 8, 11, 11, 12)
OUTER = (0, 3, 6, 8, 11, 11, 12)
GROUPS = ((0, 4), (4, 12))
F2 = 3
FAR_FIRST = (4, 3, 5, 2, 6, 1, 7)
viscosity = 0.05
mixing = 0.1
rotation = 0.2
continuity = 0.5
pressure = 0.5


def up8(n):
    return (n + 7) // 8 * 8


def tiles_of(value):
    return [value[:, t * T : (t + 1) * T] for t in range(value.shape[1] // T)]


def shift_lanes(x, by):
    return pltpu.roll(x, by % x.shape[1], 1)


def shift_rows(x, by):
    return pltpu.roll(x, by % x.shape[0], 0)


def ring_extended(x):
    w = x.shape[1]
    return with_rim(x, shift_rows(x[:, w - T :], 1), shift_rows(x[:, :T], -1))


def with_rim(x, before, after):
    low = lax.broadcasted_iota(jnp.int32, before.shape, 1) < T // 2
    return jnp.concatenate([x, jnp.where(low, after, before)], axis=1)


def dx12(q):
    return shift_lanes(q, 2) - shift_lanes(q, -2) + 8.0 * (shift_lanes(q, -1) - shift_lanes(q, 1))


def dy12(q0, q1):
    u0, u1 = shift_rows(q0, -1), shift_rows(q1, -1)
    d0, d1 = shift_rows(q0, 1), shift_rows(q1, 1)
    return d0 - u0 + 8.0 * (q1 - d1), d1 - u1 + 8.0 * (u0 - q0)


def kernel(
    NB, NS, K, NL,
    t_hbm, c_hbm, e_hbm, n_hbm, l_hbm, h_hbm,
    eo, no, so,
    thick, cor, e_in, n_in, lin, hin, lev, M, RP, RN, ST, fs, fr, ds_, dr, FB, EO, EI, G, HX, cs, cr, X, inv,
    LP, LN, levx, PP, PN, QP, QN,
    in_sem, h_sem, bulk_sem, a2a_sem, z_sem, x_sem, n_sem,
):
    W = NL // NS
    TT = W // T
    L = W + T
    QF, QD, QC = up8((TT + 1) * 4), up8((TT + 1) * 2), up8(TT * 4)
    PK = 2 * NL // T
    b = lax.axis_index("blk")
    s = lax.axis_index("sub")
    flat = b * NS + s
    total = NB * NS
    prev = lax.rem(flat + total - 1, total)
    nxt = lax.rem(flat + 1, total)
    prev = (lax.div(prev, NS), lax.rem(prev, NS))
    nxt = (lax.div(nxt, NS), lax.rem(nxt, NS))
    zup = (lax.rem(b + 1, NB), s)
    zdn = (lax.rem(b + NB - 1, NB), s)
    peers = [(b, lax.rem(s + j, NS)) for j in range(1, NS)]
    has_prev, has_next = flat > 0, flat < total - 1
    has_dn, has_up = b > 0, b < NB - 1
    one = lambda there: jnp.where(there, 1, 0)

    barrier = pltpu.get_barrier_semaphore()
    for there, peer in ((has_prev, prev), (has_next, nxt), (has_dn, zdn), (has_up, zup)):

        @pl.when(there)
        def _():
            pl.semaphore_signal(barrier, inc=1, device_id=peer, device_id_type=MESH)

    for peer in peers:
        pl.semaphore_signal(barrier, inc=1, device_id=peer, device_id_type=MESH)

    loads = [
        pltpu.make_async_copy(l_hbm, lin, in_sem.at[0]),
        pltpu.make_async_copy(t_hbm, thick, in_sem.at[1]),
        pltpu.make_async_copy(c_hbm, cor, in_sem.at[2]),
    ]
    flow_loads = [
        pltpu.make_async_copy(
            hbm.at[pl.ds(k * PK, (m - k) * PK), :], vmem, sem
        )
        for i, (k, m) in enumerate(GROUPS)
        for hbm, vmem, sem in (
            (e_hbm, e_in[i], in_sem.at[3 + i]),
            (n_hbm, n_in[i], in_sem.at[3 + len(GROUPS) + i]),
        )
    ]
    h_loads = [
        pltpu.make_async_copy(
            h_hbm.at[:, pl.ds(t * T, T)], hin.at[pl.ds(t * 16, 16), :], h_sem.at[t]
        )
        for t in range(TT)
    ]
    for c in loads + flow_loads + h_loads:
        c.start()
    def clear(there, refs):
        @pl.when(jnp.logical_not(there))
        def _():
            for ref in refs:
                ref[...] = jnp.zeros(ref.shape, ref.dtype)

    clear(has_prev, [QP, LP])
    clear(has_next, [QN, LN])
    clear(has_dn, [G.at[i, j, pl.ds(0, 8)] for i in range(2) for j in range(2)])
    clear(has_up, [G.at[i, j, pl.ds(16, 8)] for i in range(2) for j in range(2)])
    clear(has_dn, [FB.at[j, pl.ds(0, 8)] for j in range(2)] + [EI.at[0]])
    clear(has_up, [FB.at[j, pl.ds(16, 8)] for j in range(2)] + [EI.at[1]])
    for there, buf in ((has_prev, RP), (has_next, RN)):

        @pl.when(jnp.logical_not(there))
        def _():
            def zero_level(k, _):
                for f in range(2):
                    for r in range(2):
                        buf[k, f, r] = jnp.zeros((8, W), jnp.float32)
                return 0

            lax.fori_loop(0, K, zero_level, 0)

    pl.semaphore_wait(barrier, NS - 1 + one(has_prev) + one(has_next) + one(has_dn) + one(has_up))

    def to_neighbours(src_up, src_down, dst_from_prev, dst_from_next, which):
        return [
            (
                out,
                back,
                pltpu.make_async_remote_copy(
                    src_ref=src,
                    dst_ref=dst,
                    send_sem=n_sem.at[which, 0, i],
                    recv_sem=n_sem.at[which, 1, i],
                    device_id=peer,
                    device_id_type=MESH,
                ),
            )
            for i, (src, dst, peer, out, back) in enumerate(
                (
                    (src_up, dst_from_prev, nxt, has_next, has_prev),
                    (src_down, dst_from_next, prev, has_prev, has_next),
                )
            )
        ]

    def start_if(copies):
        for out, _, c in copies:
            pl.when(out)(c.start)

    def wait_recv_if(copies):
        for _, back, c in copies:
            pl.when(back)(c.wait_recv)

    def wait_send_if(copies):
        for out, _, c in copies:
            pl.when(out)(c.wait_send)

    l_copies = to_neighbours(l_hbm, l_hbm, LP, LN, 0)
    start_if(l_copies)

    def a2a(src, dst, q, which):
        out = []
        for j in FAR_FIRST:
            to = lax.rem(s + j, NS)
            out.append(
                pltpu.make_async_remote_copy(
                    src_ref=src.at[pl.ds(pl.multiple_of(to * q, 8), q), :],
                    dst_ref=dst.at[pl.ds(pl.multiple_of(s * q, 8), q), :],
                    send_sem=a2a_sem.at[which, 0, j - 1],
                    recv_sem=a2a_sem.at[which, 1, j - 1],
                    device_id=(b, to),
                    device_id_type=MESH,
                )
            )
        return out

    def own(src, dst, q):
        at = pl.ds(pl.multiple_of(s * q, 8), q)
        dst[at, :] = src[at, :]

    for c in loads:
        c.wait()
    levs = []
    for r in range(2):
        v = jnp.concatenate([lin[pl.ds(t * 2 + r, 8, stride=2 * TT), :] for t in range(TT)], axis=1)
        lev[r] = v
        levs.append(v)
    for r in range(2):
        acc = jnp.zeros((8, W), jnp.float32)
        for k in range(K):
            acc = acc + jnp.where(levs[r] > k, thick[k], 0.0)
        inv[r] = jnp.where(levs[r] > 0, 1.0 / jnp.where(levs[r] > 0, acc, 1.0), 0.0)
        ext = ring_extended(acc)
        for t, v in enumerate(tiles_of(ext)):
            ds_[pl.ds(t * 2 + r, 8, stride=QD), :] = v
    for c in h_loads:
        c.wait()
    for r in range(2):
        for t in range(TT):
            G[0, r, 8:16, t * T : (t + 1) * T] = hin[pl.ds(t * 16 + r, 8, stride=2), :]
    d_copies = a2a(ds_, dr, QD, 0)
    for c in d_copies:
        c.start()
    right, left = (b, lax.rem(s + 1, NS)), (b, lax.rem(s + NS - 1, NS))
    h_copies = [
        pltpu.make_async_remote_copy(
            src_ref=G.at[0, :, pl.ds(8, 8), pl.ds(at, T)],
            dst_ref=HX.at[i],
            send_sem=x_sem.at[0, i],
            recv_sem=x_sem.at[1, i],
            device_id=peer,
            device_id_type=MESH,
        )
        for i, (at, peer) in enumerate(((W - T, right), (0, left)))
    ]
    for c in h_copies:
        c.start()

    def bulk(k, way):
        return pltpu.make_async_remote_copy(
            src_ref=M.at[k],
            dst_ref=(RN if way == 0 else RP).at[k],
            send_sem=bulk_sem.at[way, 0, k],
            recv_sem=bulk_sem.at[way, 1, k],
            device_id=prev if way == 0 else nxt,
            device_id_type=MESH,
        )

    def start_bulk(stage):
        def some(there, way, plan):
            @pl.when(there)
            def _():
                for k in range(plan[stage], plan[stage + 1]):
                    bulk(k, way).start()

        some(s > 0, 0, INNER)
        some(jnp.logical_and(s == 0, has_prev), 0, OUTER)
        some(s < NS - 1, 1, INNER)
        some(jnp.logical_and(s == NS - 1, has_next), 1, OUTER)

    def mask_level(first, sources):
        def level(k, _):
            for r in range(2):
                wet = lev[r] > k
                for f, src in enumerate(sources):
                    at = (k - first) * PK + r
                    v = jnp.concatenate(
                        [src[pl.ds(at + t * 2, 8, stride=2 * TT), :] for t in range(TT)], axis=1
                    )
                    M[k, f, r] = jnp.where(wet, v, 0.0)
            return 0

        return level

    for i, (k, m) in enumerate(GROUPS):
        flow_loads[2 * i].wait()
        flow_loads[2 * i + 1].wait()
        lax.fori_loop(k, m, mask_level(k, (e_in[i], n_in[i])), 0)
        if i == 0:
            start_bulk(0)

    own(ds_, dr, QD)

    cv = viscosity / 12.0

    def local_level(k, sums):
        above = jnp.maximum(k - 1, 0)
        below = jnp.minimum(k + 1, K - 1)
        th = thick[k]
        out = []
        for f in range(2):
            for r in range(2):
                turn = rotation * cor[r]
                x = M[k, f, r]
                ext = ring_extended(x)
                near = (shift_lanes(ext, 1) + shift_lanes(ext, -1))[:, :W] + M[k, f, 1 - r]
                far = (shift_lanes(ext, 2) + shift_lanes(ext, -2))[:, :W]
                lap = 16.0 * near - far
                vz = M[above, f, r] + M[below, f, r]
                other = M[k, 1 - f, r]
                sign = turn if f == 0 else -turn
                v = (1.0 - 60.0 * cv - 2.0 * mixing) * x + cv * lap + mixing * vz + sign * other
                ST[k, f, r] = v
                out.append(sums[2 * f + r] + jnp.where(lev[r] > k, th * v, 0.0))
        return tuple(out)

    zeros = tuple(jnp.zeros((8, W), jnp.float32) for _ in range(4))
    sums = lax.fori_loop(0, K // 2, local_level, zeros)

    wait_recv_if(l_copies)
    for i, src in ((0, LP), (1, LN)):
        for r in range(2):
            levx[i, r] = jnp.concatenate(
                [src[pl.ds(t * 2 + r, 8, stride=2 * TT), :] for t in range(TT)], axis=1
            )

    def partial_level(i):
        def level(k, sums):
            th = thick[k]
            wet = [levx[i, r] > k for r in range(2)]
            out = []
            for f in range(2):
                m0, m1 = M[k, f, 0], M[k, f, 1]
                terms = (-m0, 16.0 * m0 - m1) if i == 0 else (16.0 * m1 - m0, -m1)
                for r in range(2):
                    out.append(sums[2 * f + r] + jnp.where(wet[r], th * terms[r], 0.0))
            return tuple(out)

        return level

    for i, dst in ((0, PP), (1, PN)):
        part = lax.fori_loop(0, K, partial_level(i), zeros)
        for f in range(2):
            for r in range(2):
                dst[f, r] = part[2 * f + r]
    p_copies = to_neighbours(PN, PP, QP, QN, 1)
    start_if(p_copies)
    start_bulk(1)
    sums = lax.fori_loop(K // 2, K, local_level, sums)

    for c in d_copies + h_copies:
        c.wait_recv()
    for r in range(2):
        G[0, r, 8:16, W:L] = with_rim(HX[1, r], HX[0, r], HX[1, r])[:, T:]
        for t in range(TT + 1):
            G[1, r, 8:16, t * T : (t + 1) * T] = dr[pl.ds(t * 2 + r, 8, stride=QD), :]

    def zcopies(which, of):
        return [
            (
                out,
                back,
                pltpu.make_async_remote_copy(
                    src_ref=of(i, 8)[0],
                    dst_ref=of(i, to)[1],
                    send_sem=z_sem.at[which, 0, i],
                    recv_sem=z_sem.at[which, 1, i],
                    device_id=peer,
                    device_id_type=MESH,
                ),
            )
            for i, (to, peer, out, back) in enumerate(((0, zup, has_up, has_dn), (16, zdn, has_dn, has_up)))
        ]

    g_copies = zcopies(0, lambda i, to: [G.at[:, :, pl.ds(to, 8), :]] * 2)
    start_if(g_copies)

    wait_recv_if(p_copies)
    for f in range(2):
        for r in range(2):
            v = sums[2 * f + r] + cv * QP[f, r] + cv * QN[f, r]
            for t, v in enumerate(tiles_of(ring_extended(v))):
                fs[pl.ds(t * 4 + f * 2 + r, 8, stride=QF), :] = v
    f_copies = a2a(fs, fr, QF, 1)
    for c in f_copies:
        c.start()
    start_bulk(2)
    own(fs, fr, QF)

    def finish_level(k, _):
        pl.when(has_next)(bulk(k, 0).wait_recv)
        pl.when(has_prev)(bulk(k, 1).wait_recv)
        for f in range(2):
            p0, p1 = RP[k, f, 0], RP[k, f, 1]
            n0, n1 = RN[k, f, 0], RN[k, f, 1]
            for r in range(2):
                if r == 0:
                    add = cv * (16.0 * p1 - p0) - cv * n0
                else:
                    add = cv * (16.0 * n0 - n1) - cv * p1
                ST[k, f, r] = ST[k, f, r] + add
        return 0

    for c in f_copies:
        c.wait_recv()
    east, north = [
        [
            jnp.concatenate([fr[pl.ds(t * 4 + f * 2 + r, 8, stride=QF), :] for t in range(TT + 1)], axis=1)
            for r in range(2)
        ]
        for f in range(2)
    ]
    for r in range(2):
        for t, v in enumerate(tiles_of(north[r])):
            EO[0, r * (TT + 1) + t : r * (TT + 1) + t + 1, :] = v[7:8]
            EO[1, r * (TT + 1) + t : r * (TT + 1) + t + 1, :] = v[0:1]
    none = jnp.zeros((8, L), jnp.float32)
    across = dy12(*[jnp.concatenate([none, v, none], axis=0) for v in north])
    for r in range(2):
        FB[r, 8:16, :] = dx12(east[r]) + across[r][8:16]
    b_copies = zcopies(1, lambda i, to: [FB.at[:, pl.ds(to, 8), :]] * 2)
    b_copies += zcopies(2, lambda i, to: [EO.at[i], EI.at[i]])
    start_if(b_copies)
    start_bulk(3)
    lax.fori_loop(0, F2, finish_level, 0)
    wait_recv_if(g_copies)
    wait_recv_if(b_copies)
    start_bulk(4)

    row = lax.broadcasted_iota(jnp.int32, (24, T), 0)
    inside = jnp.logical_and(jnp.logical_or(row >= 8, has_dn), jnp.logical_or(row < 16, has_up))
    step = jnp.concatenate([jnp.where(inside, continuity / 12.0, 0.0)] * (TT + 1), axis=1)
    high = [G[0, r] for r in range(2)]
    deep = [G[1, r] * (pressure / 12.0) for r in range(2)]
    edge = [
        jnp.concatenate(
            [
                jnp.where(
                    row == 7,
                    EI[0, r * (TT + 1) + t : r * (TT + 1) + t + 1, :],
                    jnp.where(row == 16, EI[1, r * (TT + 1) + t : r * (TT + 1) + t + 1, :], 0.0),
                )
                for t in range(TT + 1)
            ],
            axis=1,
        )
        for r in range(2)
    ]
    edge = dy12(edge[0], edge[1])
    flow = [
        step
        * (
            FB[r]
            + jnp.concatenate([across[r][:8], edge[r][8:16], across[r][16:]], axis=0)
        )
        for r in range(2)
    ]
    high = [high[r] - flow[r] for r in range(2)]
    dh = dy12(high[0], high[1])
    east = [-deep[r] * dx12(high[r]) for r in range(2)]
    north = [-deep[r] * dh[r] for r in range(2)]
    for _ in range(NSUB - 1):
        dn = dy12(north[0], north[1])
        high = [high[r] - flow[r] - step * (dx12(east[r]) + dn[r]) for r in range(2)]
        dh = dy12(high[0], high[1])
        east = [east[r] - deep[r] * dx12(high[r]) for r in range(2)]
        north = [north[r] - deep[r] * dh[r] for r in range(2)]
    for f, field in ((0, east), (1, north)):
        for r in range(2):
            for t, v in enumerate(tiles_of(field[r][8:16, :W])):
                cs[pl.ds(t * 4 + f * 2 + r, 8, stride=QC), :] = v
    c_copies = a2a(cs, cr, QC, 2)
    for c in c_copies:
        c.start()
    start_bulk(5)
    for r in range(2):
        for t in range(TT):
            so[pl.ds(t * 16 + r, 8, stride=2), :] = high[r][8:16, t * T : (t + 1) * T]
    own(cs, cr, QC)
    lax.fori_loop(F2, K, finish_level, 0)
    for c in c_copies:
        c.wait_recv()
    for f in range(2):
        for r in range(2):
            v = jnp.concatenate(
                [cr[pl.ds(t * 4 + f * 2 + r, 8, stride=QC), :] for t in range(TT)], axis=1
            )
            X[f, r] = v * inv[r]

    def store_level(k, _):
        for r in range(2):
            wet = lev[r] > k
            for f, dst in ((0, eo), (1, no)):
                v = jnp.where(wet, ST[k, f, r] + X[f, r], 0.0)
                for t in range(TT):
                    dst[pl.ds(k * PK + t * 2 + r, 8, stride=2 * TT), :] = v[:, t * T : (t + 1) * T]
        return 0

    lax.fori_loop(0, K, store_level, 0)

    def drain(k, _):
        pl.when(has_prev)(bulk(k, 0).wait_send)
        pl.when(has_next)(bulk(k, 1).wait_send)
        return 0

    lax.fori_loop(0, K, drain, 0)
    for c in d_copies + h_copies + f_copies + c_copies:
        c.wait_send()
    for c in (l_copies, p_copies, g_copies, b_copies):
        wait_send_if(c)


def store_kernel(e, n, h, eo, no, ho, sem, h_sem):
    TT = ho.shape[1] // T
    copies = [pltpu.make_async_copy(e, eo, sem.at[0]), pltpu.make_async_copy(n, no, sem.at[1])]
    copies += [
        pltpu.make_async_copy(h.at[pl.ds(t * 16, 16), :], ho.at[:, pl.ds(t * T, T)], h_sem.at[t])
        for t in range(TT)
    ]
    for c in copies:
        c.start()
    for c in copies:
        c.wait()


def flattened(x):
    k = x.shape[1]
    x = x.reshape(2, k, -1, T).transpose(1, 2, 0, 3)
    return x.reshape(-1, T)


def unflattened(x, k):
    x = x.reshape(k, -1, 2, T).transpose(2, 0, 1, 3)
    return x.reshape(2, k, -1)


def body(NB, NS, east_flow, north_flow, levels, coriolis, thickness, surface):
    _, K, NL = east_flow.shape
    W = NL // NS
    TT = W // T
    L = W + T
    rows = K * 2 * NL // T
    QF, QD, QC = up8((TT + 1) * 4), up8((TT + 1) * 2), up8(TT * 4)
    f32 = jnp.float32
    lev = levels.reshape(2, -1, T).transpose(1, 0, 2).reshape(-1, T)
    any_ = pl.BlockSpec(memory_space=pl.ANY)
    hbm = pl.BlockSpec(memory_space=pltpu.HBM)
    vmem = pl.BlockSpec(memory_space=pltpu.VMEM)
    big = pltpu.VMEM((K, 2, 2, 8, W), f32)
    sums = pltpu.VMEM((2, 2, 8, W), f32)
    dma = pltpu.SemaphoreType.DMA
    eo, no, so = pl.pallas_call(
        functools.partial(kernel, NB, NS, K, NL),
        out_shape=(
            jax.ShapeDtypeStruct((rows, T), f32),
            jax.ShapeDtypeStruct((rows, T), f32),
            jax.ShapeDtypeStruct((16 * TT, T), f32),
        ),
        in_specs=[hbm] * 6,
        out_specs=[vmem] * 3,
        scratch_shapes=[
            pltpu.SMEM((K,), f32),
            pltpu.SMEM((2,), f32),
            [pltpu.VMEM(((m - k) * rows // K, T), f32) for k, m in GROUPS],
            [pltpu.VMEM(((m - k) * rows // K, T), f32) for k, m in GROUPS],
            pltpu.VMEM((2 * NL // T, T), jnp.int32),
            pltpu.VMEM((16 * TT, T), f32),
            pltpu.VMEM((2, 8, W), jnp.int32),
            big,
            big,
            big,
            big,
            pltpu.VMEM((NS * QF, T), f32),
            pltpu.VMEM((NS * QF, T), f32),
            pltpu.VMEM((NS * QD, T), f32),
            pltpu.VMEM((NS * QD, T), f32),
            pltpu.VMEM((2, 24, L), f32),
            pltpu.VMEM((2, up8(2 * (TT + 1)), T), f32),
            pltpu.VMEM((2, up8(2 * (TT + 1)), T), f32),
            pltpu.VMEM((2, 2, 24, L), f32),
            pltpu.VMEM((2, 2, 8, T), f32),
            pltpu.VMEM((NS * QC, T), f32),
            pltpu.VMEM((NS * QC, T), f32),
            sums,
            pltpu.VMEM((2, 8, W), f32),
            pltpu.VMEM((2 * NL // T, T), jnp.int32),
            pltpu.VMEM((2 * NL // T, T), jnp.int32),
            pltpu.VMEM((2, 2, 8, W), jnp.int32),
            sums,
            sums,
            sums,
            sums,
            dma((3 + 2 * len(GROUPS),)),
            dma((TT,)),
            dma((2, 2, K)),
            dma((3, 2, NS - 1)),
            dma((3, 2, 2)),
            dma((2, 2)),
            dma((2, 2, 2)),
        ],
        compiler_params=pltpu.CompilerParams(
            collective_id=0, has_side_effects=True, vmem_limit_bytes=VMEM_LIMIT
        ),
    )(*[pltpu.with_memory_space_constraint(x, pltpu.HBM) for x in (thickness, coriolis, flattened(east_flow), flattened(north_flow), lev, surface)])
    eo, no, so = pl.pallas_call(
        store_kernel,
        out_shape=(
            jax.ShapeDtypeStruct((rows, T), f32),
            jax.ShapeDtypeStruct((rows, T), f32),
            jax.ShapeDtypeStruct((16, W), f32),
        ),
        in_specs=[any_] * 3,
        out_specs=[hbm] * 3,
        scratch_shapes=[dma((2,)), dma((TT,))],
        compiler_params=pltpu.CompilerParams(vmem_limit_bytes=VMEM_LIMIT),
    )(eo, no, so)
    return unflattened(eo, K), unflattened(no, K), so


def solution(mesh):
    NB, NS = mesh.shape["blk"], mesh.shape["sub"]
    both = ("blk", "sub")
    return jax.shard_map(
        functools.partial(body, NB, NS),
        mesh=mesh,
        in_specs=(P(both, None, None), P(both, None, None), P(both, None), P(both), P(), P("blk", "sub")),
        out_specs=(P(both, None, None), P(both, None, None), P("blk", "sub")),
        check_vma=False,
    )
```

```python
import functools

import jax
import jax.numpy as jnp
from jax import lax
from jax.experimental import pallas as pl
from jax.experimental.pallas import tpu as pltpu
from jax.sharding import PartitionSpec as P

MESH = pl.DeviceIdType.MESH
T = 128
NSUB = 4
VMEM_LIMIT = 16 << 20
PARTS = 4
INNER = (0, 3, 6, 9, 12, 12, 12)
OUTER = (0, 3, 6, 9, 12, 12, 12)
GROUPS = ((0, 4), (4, 12))
F2 = 3
FAR_FIRST = (4, 3, 5, 2, 6, 1, 7)
viscosity = 0.05
mixing = 0.1
rotation = 0.2
continuity = 0.5
pressure = 0.5


def up8(n):
    return (n + 7) // 8 * 8


def tiles_of(value):
    return [value[:, t * T : (t + 1) * T] for t in range(value.shape[1] // T)]


def shift_lanes(x, by):
    return pltpu.roll(x, by % x.shape[1], 1)


def shift_rows(x, by):
    return pltpu.roll(x, by % x.shape[0], 0)


def ring_extended(x):
    w = x.shape[1]
    return with_rim(x, shift_rows(x[:, w - T :], 1), shift_rows(x[:, :T], -1))


def with_rim(x, before, after):
    low = lax.broadcasted_iota(jnp.int32, before.shape, 1) < T // 2
    return jnp.concatenate([x, jnp.where(low, after, before)], axis=1)


def dx12(q):
    return shift_lanes(q, 2) - shift_lanes(q, -2) + 8.0 * (shift_lanes(q, -1) - shift_lanes(q, 1))


def dy12(q0, q1):
    u0, u1 = shift_rows(q0, -1), shift_rows(q1, -1)
    d0, d1 = shift_rows(q0, 1), shift_rows(q1, 1)
    return d0 - u0 + 8.0 * (q1 - d1), d1 - u1 + 8.0 * (u0 - q0)


def kernel(
    NB, NS, K, NL,
    t_hbm, c_hbm, e_hbm, n_hbm, l_hbm, h_hbm,
    ST, X, lev, so,
    thick, cor, e_in, n_in, lin, hin, M, RP, RN, fs, fr, ds_, dr, FB, EO, EI, G, HX, cs, cr, inv,
    LP, LN, levx, PP, PN, QP, QN,
    in_sem, h_sem, bulk_sem, a2a_sem, z_sem, x_sem, n_sem,
):
    W = NL // NS
    TT = W // T
    L = W + T
    QF, QD, QC = up8((TT + 1) * 4), up8((TT + 1) * 2), up8(TT * 4)
    PK = 2 * NL // T
    b = lax.axis_index("blk")
    s = lax.axis_index("sub")
    flat = b * NS + s
    total = NB * NS
    prev = lax.rem(flat + total - 1, total)
    nxt = lax.rem(flat + 1, total)
    prev = (lax.div(prev, NS), lax.rem(prev, NS))
    nxt = (lax.div(nxt, NS), lax.rem(nxt, NS))
    zup = (lax.rem(b + 1, NB), s)
    zdn = (lax.rem(b + NB - 1, NB), s)
    peers = [(b, lax.rem(s + j, NS)) for j in range(1, NS)]
    has_prev, has_next = flat > 0, flat < total - 1
    has_dn, has_up = b > 0, b < NB - 1
    one = lambda there: jnp.where(there, 1, 0)

    barrier = pltpu.get_barrier_semaphore()
    for there, peer in ((has_prev, prev), (has_next, nxt), (has_dn, zdn), (has_up, zup)):

        @pl.when(there)
        def _():
            pl.semaphore_signal(barrier, inc=1, device_id=peer, device_id_type=MESH)

    for peer in peers:
        pl.semaphore_signal(barrier, inc=1, device_id=peer, device_id_type=MESH)

    loads = [
        pltpu.make_async_copy(l_hbm, lin, in_sem.at[0]),
        pltpu.make_async_copy(t_hbm, thick, in_sem.at[1]),
        pltpu.make_async_copy(c_hbm, cor, in_sem.at[2]),
    ]
    flow_loads = [
        pltpu.make_async_copy(
            hbm.at[pl.ds(k * PK, (m - k) * PK), :], vmem, sem
        )
        for i, (k, m) in enumerate(GROUPS)
        for hbm, vmem, sem in (
            (e_hbm, e_in[i], in_sem.at[3 + i]),
            (n_hbm, n_in[i], in_sem.at[3 + len(GROUPS) + i]),
        )
    ]
    h_loads = [
        pltpu.make_async_copy(
            h_hbm.at[:, pl.ds(t * T, T)], hin.at[pl.ds(t * 16, 16), :], h_sem.at[t]
        )
        for t in range(TT)
    ]
    for c in loads + flow_loads + h_loads:
        c.start()
    def clear(there, refs):
        @pl.when(jnp.logical_not(there))
        def _():
            for ref in refs:
                ref[...] = jnp.zeros(ref.shape, ref.dtype)

    clear(has_prev, [QP, LP])
    clear(has_next, [QN, LN])
    clear(has_dn, [G.at[i, j, pl.ds(0, 8)] for i in range(2) for j in range(2)])
    clear(has_up, [G.at[i, j, pl.ds(16, 8)] for i in range(2) for j in range(2)])
    clear(has_dn, [FB.at[j, pl.ds(0, 8)] for j in range(2)] + [EI.at[0]])
    clear(has_up, [FB.at[j, pl.ds(16, 8)] for j in range(2)] + [EI.at[1]])
    for there, buf in ((has_prev, RP), (has_next, RN)):

        @pl.when(jnp.logical_not(there))
        def _():
            def zero_level(k, _):
                for f in range(2):
                    for r in range(2):
                        buf[k, f, r] = jnp.zeros((8, W), jnp.float32)
                return 0

            lax.fori_loop(0, K, zero_level, 0)

    pl.semaphore_wait(barrier, NS - 1 + one(has_prev) + one(has_next) + one(has_dn) + one(has_up))

    def to_neighbours(src_up, src_down, dst_from_prev, dst_from_next, which):
        return [
            (
                out,
                back,
                pltpu.make_async_remote_copy(
                    src_ref=src,
                    dst_ref=dst,
                    send_sem=n_sem.at[which, 0, i],
                    recv_sem=n_sem.at[which, 1, i],
                    device_id=peer,
                    device_id_type=MESH,
                ),
            )
            for i, (src, dst, peer, out, back) in enumerate(
                (
                    (src_up, dst_from_prev, nxt, has_next, has_prev),
                    (src_down, dst_from_next, prev, has_prev, has_next),
                )
            )
        ]

    def start_if(copies):
        for out, _, c in copies:
            pl.when(out)(c.start)

    def wait_recv_if(copies):
        for _, back, c in copies:
            pl.when(back)(c.wait_recv)

    def wait_send_if(copies):
        for out, _, c in copies:
            pl.when(out)(c.wait_send)

    l_copies = to_neighbours(l_hbm, l_hbm, LP, LN, 0)
    start_if(l_copies)

    def a2a(src, dst, q, which):
        out = []
        for j in FAR_FIRST:
            to = lax.rem(s + j, NS)
            out.append(
                pltpu.make_async_remote_copy(
                    src_ref=src.at[pl.ds(pl.multiple_of(to * q, 8), q), :],
                    dst_ref=dst.at[pl.ds(pl.multiple_of(s * q, 8), q), :],
                    send_sem=a2a_sem.at[which, 0, j - 1],
                    recv_sem=a2a_sem.at[which, 1, j - 1],
                    device_id=(b, to),
                    device_id_type=MESH,
                )
            )
        return out

    def own(src, dst, q):
        at = pl.ds(pl.multiple_of(s * q, 8), q)
        dst[at, :] = src[at, :]

    for c in loads:
        c.wait()
    levs = []
    for r in range(2):
        v = jnp.concatenate([lin[pl.ds(t * 2 + r, 8, stride=2 * TT), :] for t in range(TT)], axis=1)
        lev[r] = v
        levs.append(v)
    for r in range(2):
        acc = jnp.zeros((8, W), jnp.float32)
        for k in range(K):
            acc = acc + jnp.where(levs[r] > k, thick[k], 0.0)
        inv[r] = jnp.where(levs[r] > 0, 1.0 / jnp.where(levs[r] > 0, acc, 1.0), 0.0)
        ext = ring_extended(acc)
        for t, v in enumerate(tiles_of(ext)):
            ds_[pl.ds(t * 2 + r, 8, stride=QD), :] = v
    for c in h_loads:
        c.wait()
    for r in range(2):
        for t in range(TT):
            G[0, r, 8:16, t * T : (t + 1) * T] = hin[pl.ds(t * 16 + r, 8, stride=2), :]
    d_copies = a2a(ds_, dr, QD, 0)
    for c in d_copies:
        c.start()
    right, left = (b, lax.rem(s + 1, NS)), (b, lax.rem(s + NS - 1, NS))
    h_copies = [
        pltpu.make_async_remote_copy(
            src_ref=G.at[0, :, pl.ds(8, 8), pl.ds(at, T)],
            dst_ref=HX.at[i],
            send_sem=x_sem.at[0, i],
            recv_sem=x_sem.at[1, i],
            device_id=peer,
            device_id_type=MESH,
        )
        for i, (at, peer) in enumerate(((W - T, right), (0, left)))
    ]
    for c in h_copies:
        c.start()

    def bulk(k, way):
        return pltpu.make_async_remote_copy(
            src_ref=M.at[k],
            dst_ref=(RN if way == 0 else RP).at[k],
            send_sem=bulk_sem.at[way, 0, k],
            recv_sem=bulk_sem.at[way, 1, k],
            device_id=prev if way == 0 else nxt,
            device_id_type=MESH,
        )

    def start_bulk(stage):
        def some(there, way, plan):
            @pl.when(there)
            def _():
                for k in range(plan[stage], plan[stage + 1]):
                    bulk(k, way).start()

        some(s > 0, 0, INNER)
        some(jnp.logical_and(s == 0, has_prev), 0, OUTER)
        some(s < NS - 1, 1, INNER)
        some(jnp.logical_and(s == NS - 1, has_next), 1, OUTER)

    def mask_level(first, sources):
        def level(k, _):
            for r in range(2):
                wet = lev[r] > k
                for f, src in enumerate(sources):
                    at = (k - first) * PK + r
                    v = jnp.concatenate(
                        [src[pl.ds(at + t * 2, 8, stride=2 * TT), :] for t in range(TT)], axis=1
                    )
                    M[k, f, r] = jnp.where(wet, v, 0.0)
            return 0

        return level

    for i, (k, m) in enumerate(GROUPS):
        flow_loads[2 * i].wait()
        flow_loads[2 * i + 1].wait()
        lax.fori_loop(k, m, mask_level(k, (e_in[i], n_in[i])), 0)
        if i == 0:
            start_bulk(0)

    own(ds_, dr, QD)

    cv = viscosity / 12.0

    def local_level(k, sums):
        above = jnp.maximum(k - 1, 0)
        below = jnp.minimum(k + 1, K - 1)
        th = thick[k]
        out = []
        for f in range(2):
            for r in range(2):
                turn = rotation * cor[r]
                x = M[k, f, r]
                ext = ring_extended(x)
                near = (shift_lanes(ext, 1) + shift_lanes(ext, -1))[:, :W] + M[k, f, 1 - r]
                far = (shift_lanes(ext, 2) + shift_lanes(ext, -2))[:, :W]
                lap = 16.0 * near - far
                vz = M[above, f, r] + M[below, f, r]
                other = M[k, 1 - f, r]
                sign = turn if f == 0 else -turn
                v = (1.0 - 60.0 * cv - 2.0 * mixing) * x + cv * lap + mixing * vz + sign * other
                ST[k, f, r] = v
                out.append(sums[2 * f + r] + jnp.where(lev[r] > k, th * v, 0.0))
        return tuple(out)

    zeros = tuple(jnp.zeros((8, W), jnp.float32) for _ in range(4))
    sums = lax.fori_loop(0, K // 3, local_level, zeros)

    wait_recv_if(l_copies)
    for i, src in ((0, LP), (1, LN)):
        for r in range(2):
            levx[i, r] = jnp.concatenate(
                [src[pl.ds(t * 2 + r, 8, stride=2 * TT), :] for t in range(TT)], axis=1
            )

    def partial_level(i):
        def level(k, sums):
            th = thick[k]
            wet = [levx[i, r] > k for r in range(2)]
            out = []
            for f in range(2):
                m0, m1 = M[k, f, 0], M[k, f, 1]
                terms = (-m0, 16.0 * m0 - m1) if i == 0 else (16.0 * m1 - m0, -m1)
                for r in range(2):
                    out.append(sums[2 * f + r] + jnp.where(wet[r], th * terms[r], 0.0))
            return tuple(out)

        return level

    for i, dst in ((0, PP), (1, PN)):
        part = lax.fori_loop(0, K, partial_level(i), zeros)
        for f in range(2):
            for r in range(2):
                dst[f, r] = part[2 * f + r]
    p_copies = to_neighbours(PN, PP, QP, QN, 1)
    start_if(p_copies)
    start_bulk(1)
    sums = lax.fori_loop(K // 3, K, local_level, sums)

    for c in d_copies + h_copies:
        c.wait_recv()
    for r in range(2):
        G[0, r, 8:16, W:L] = with_rim(HX[1, r], HX[0, r], HX[1, r])[:, T:]
        for t in range(TT + 1):
            G[1, r, 8:16, t * T : (t + 1) * T] = dr[pl.ds(t * 2 + r, 8, stride=QD), :]

    def zcopies(which, of):
        return [
            (
                out,
                back,
                pltpu.make_async_remote_copy(
                    src_ref=of(i, 8)[0],
                    dst_ref=of(i, to)[1],
                    send_sem=z_sem.at[which, 0, i],
                    recv_sem=z_sem.at[which, 1, i],
                    device_id=peer,
                    device_id_type=MESH,
                ),
            )
            for i, (to, peer, out, back) in enumerate(((0, zup, has_up, has_dn), (16, zdn, has_dn, has_up)))
        ]

    g_copies = zcopies(0, lambda i, to: [G.at[:, :, pl.ds(to, 8), :]] * 2)
    start_if(g_copies)

    wait_recv_if(p_copies)
    for f in range(2):
        for r in range(2):
            v = sums[2 * f + r] + cv * QP[f, r] + cv * QN[f, r]
            for t, v in enumerate(tiles_of(ring_extended(v))):
                fs[pl.ds(t * 4 + f * 2 + r, 8, stride=QF), :] = v
    f_copies = a2a(fs, fr, QF, 1)
    for c in f_copies:
        c.start()
    start_bulk(2)
    own(fs, fr, QF)

    def finish_level(k, _):
        pl.when(has_next)(bulk(k, 0).wait_recv)
        pl.when(has_prev)(bulk(k, 1).wait_recv)
        for f in range(2):
            p0, p1 = RP[k, f, 0], RP[k, f, 1]
            n0, n1 = RN[k, f, 0], RN[k, f, 1]
            for r in range(2):
                if r == 0:
                    add = cv * (16.0 * p1 - p0) - cv * n0
                else:
                    add = cv * (16.0 * n0 - n1) - cv * p1
                ST[k, f, r] = ST[k, f, r] + add
        return 0

    for c in f_copies:
        c.wait_recv()
    east, north = [
        [
            jnp.concatenate([fr[pl.ds(t * 4 + f * 2 + r, 8, stride=QF), :] for t in range(TT + 1)], axis=1)
            for r in range(2)
        ]
        for f in range(2)
    ]
    for r in range(2):
        for t, v in enumerate(tiles_of(north[r])):
            EO[0, r * (TT + 1) + t : r * (TT + 1) + t + 1, :] = v[7:8]
            EO[1, r * (TT + 1) + t : r * (TT + 1) + t + 1, :] = v[0:1]
    none = jnp.zeros((8, L), jnp.float32)
    across = dy12(*[jnp.concatenate([none, v, none], axis=0) for v in north])
    for r in range(2):
        FB[r, 8:16, :] = dx12(east[r]) + across[r][8:16]
    b_copies = zcopies(1, lambda i, to: [FB.at[:, pl.ds(to, 8), :]] * 2)
    b_copies += zcopies(2, lambda i, to: [EO.at[i], EI.at[i]])
    start_if(b_copies)
    start_bulk(3)
    lax.fori_loop(0, F2, finish_level, 0)
    wait_recv_if(g_copies)
    wait_recv_if(b_copies)
    start_bulk(4)

    row = lax.broadcasted_iota(jnp.int32, (24, T), 0)
    inside = jnp.logical_and(jnp.logical_or(row >= 8, has_dn), jnp.logical_or(row < 16, has_up))
    step = jnp.concatenate([jnp.where(inside, continuity / 12.0, 0.0)] * (TT + 1), axis=1)
    high = [G[0, r] for r in range(2)]
    deep = [G[1, r] * (pressure / 12.0) for r in range(2)]
    edge = [
        jnp.concatenate(
            [
                jnp.where(
                    row == 7,
                    EI[0, r * (TT + 1) + t : r * (TT + 1) + t + 1, :],
                    jnp.where(row == 16, EI[1, r * (TT + 1) + t : r * (TT + 1) + t + 1, :], 0.0),
                )
                for t in range(TT + 1)
            ],
            axis=1,
        )
        for r in range(2)
    ]
    edge = dy12(edge[0], edge[1])
    flow = [
        step
        * (
            FB[r]
            + jnp.concatenate([across[r][:8], edge[r][8:16], across[r][16:]], axis=0)
        )
        for r in range(2)
    ]
    high = [high[r] - flow[r] for r in range(2)]
    dh = dy12(high[0], high[1])
    east = [-deep[r] * dx12(high[r]) for r in range(2)]
    north = [-deep[r] * dh[r] for r in range(2)]
    for _ in range(NSUB - 1):
        dn = dy12(north[0], north[1])
        high = [high[r] - flow[r] - step * (dx12(east[r]) + dn[r]) for r in range(2)]
        dh = dy12(high[0], high[1])
        east = [east[r] - deep[r] * dx12(high[r]) for r in range(2)]
        north = [north[r] - deep[r] * dh[r] for r in range(2)]
    for f, field in ((0, east), (1, north)):
        for r in range(2):
            for t, v in enumerate(tiles_of(field[r][8:16, :W])):
                cs[pl.ds(t * 4 + f * 2 + r, 8, stride=QC), :] = v
    c_copies = a2a(cs, cr, QC, 2)
    for c in c_copies:
        c.start()
    start_bulk(5)
    for r in range(2):
        for t in range(TT):
            so[pl.ds(t * 16 + r, 8, stride=2), :] = high[r][8:16, t * T : (t + 1) * T]
    own(cs, cr, QC)
    lax.fori_loop(F2, K, finish_level, 0)
    for c in c_copies:
        c.wait_recv()
    for f in range(2):
        for r in range(2):
            v = jnp.concatenate(
                [cr[pl.ds(t * 4 + f * 2 + r, 8, stride=QC), :] for t in range(TT)], axis=1
            )
            X[f, r] = v * inv[r]

    def drain(k, _):
        pl.when(has_prev)(bulk(k, 0).wait_send)
        pl.when(has_next)(bulk(k, 1).wait_send)
        return 0

    lax.fori_loop(0, K, drain, 0)
    for c in d_copies + h_copies + f_copies + c_copies:
        c.wait_send()
    for c in (l_copies, p_copies, g_copies, b_copies):
        wait_send_if(c)


def store_kernel(ST, X, lev, h, eo_hbm, no_hbm, ho, eo, no, sem, h_sem):
    K, W = ST.shape[0], ST.shape[-1]
    TT = W // T
    PK = eo_hbm.shape[0] // K
    part = K // PARTS
    copies = [
        pltpu.make_async_copy(h.at[pl.ds(t * 16, 16), :], ho.at[:, pl.ds(t * T, T)], h_sem.at[t])
        for t in range(TT)
    ]
    for c in copies:
        c.start()

    def store_level(first, dsts):
        def level(k, _):
            for r in range(2):
                wet = lev[r] > k
                for f, dst in enumerate(dsts):
                    v = jnp.where(wet, ST[k, f, r] + X[f, r], 0.0)
                    at = (k - first) * PK + r
                    for t in range(TT):
                        dst[pl.ds(at + t * 2, 8, stride=2 * TT), :] = v[:, t * T : (t + 1) * T]
            return 0

        return level

    for i in range(PARTS):
        first = i * part
        lax.fori_loop(first, first + part, store_level(first, (eo[i], no[i])), 0)
        for f, (src, dst) in enumerate(((eo[i], eo_hbm), (no[i], no_hbm))):
            c = pltpu.make_async_copy(src, dst.at[pl.ds(first * PK, part * PK), :], sem.at[f, i])
            c.start()
            copies.append(c)
    for c in copies:
        c.wait()


def flattened(x):
    k = x.shape[1]
    x = x.reshape(2, k, -1, T).transpose(1, 2, 0, 3)
    return x.reshape(-1, T)


def unflattened(x, k):
    x = x.reshape(k, -1, 2, T).transpose(2, 0, 1, 3)
    return x.reshape(2, k, -1)


def body(NB, NS, east_flow, north_flow, levels, coriolis, thickness, surface):
    _, K, NL = east_flow.shape
    W = NL // NS
    TT = W // T
    L = W + T
    rows = K * 2 * NL // T
    QF, QD, QC = up8((TT + 1) * 4), up8((TT + 1) * 2), up8(TT * 4)
    f32 = jnp.float32
    lev = levels.reshape(2, -1, T).transpose(1, 0, 2).reshape(-1, T)
    any_ = pl.BlockSpec(memory_space=pl.ANY)
    hbm = pl.BlockSpec(memory_space=pltpu.HBM)
    vmem = pl.BlockSpec(memory_space=pltpu.VMEM)
    big = pltpu.VMEM((K, 2, 2, 8, W), f32)
    sums = pltpu.VMEM((2, 2, 8, W), f32)
    dma = pltpu.SemaphoreType.DMA
    star, change, deep, so = pl.pallas_call(
        functools.partial(kernel, NB, NS, K, NL),
        out_shape=(
            jax.ShapeDtypeStruct((K, 2, 2, 8, W), f32),
            jax.ShapeDtypeStruct((2, 2, 8, W), f32),
            jax.ShapeDtypeStruct((2, 8, W), jnp.int32),
            jax.ShapeDtypeStruct((16 * TT, T), f32),
        ),
        in_specs=[hbm] * 6,
        out_specs=[vmem] * 4,
        scratch_shapes=[
            pltpu.SMEM((K,), f32),
            pltpu.SMEM((2,), f32),
            [pltpu.VMEM(((m - k) * rows // K, T), f32) for k, m in GROUPS],
            [pltpu.VMEM(((m - k) * rows // K, T), f32) for k, m in GROUPS],
            pltpu.VMEM((2 * NL // T, T), jnp.int32),
            pltpu.VMEM((16 * TT, T), f32),
            big,
            big,
            big,
            pltpu.VMEM((NS * QF, T), f32),
            pltpu.VMEM((NS * QF, T), f32),
            pltpu.VMEM((NS * QD, T), f32),
            pltpu.VMEM((NS * QD, T), f32),
            pltpu.VMEM((2, 24, L), f32),
            pltpu.VMEM((2, up8(2 * (TT + 1)), T), f32),
            pltpu.VMEM((2, up8(2 * (TT + 1)), T), f32),
            pltpu.VMEM((2, 2, 24, L), f32),
            pltpu.VMEM((2, 2, 8, T), f32),
            pltpu.VMEM((NS * QC, T), f32),
            pltpu.VMEM((NS * QC, T), f32),
            pltpu.VMEM((2, 8, W), f32),
            pltpu.VMEM((2 * NL // T, T), jnp.int32),
            pltpu.VMEM((2 * NL // T, T), jnp.int32),
            pltpu.VMEM((2, 2, 8, W), jnp.int32),
            sums,
            sums,
            sums,
            sums,
            dma((3 + 2 * len(GROUPS),)),
            dma((TT,)),
            dma((2, 2, K)),
            dma((3, 2, NS - 1)),
            dma((3, 2, 2)),
            dma((2, 2)),
            dma((2, 2, 2)),
        ],
        compiler_params=pltpu.CompilerParams(
            collective_id=0, has_side_effects=True, vmem_limit_bytes=VMEM_LIMIT
        ),
    )(*[pltpu.with_memory_space_constraint(x, pltpu.HBM) for x in (thickness, coriolis, flattened(east_flow), flattened(north_flow), lev, surface)])
    eo, no, so = pl.pallas_call(
        store_kernel,
        out_shape=(
            jax.ShapeDtypeStruct((rows, T), f32),
            jax.ShapeDtypeStruct((rows, T), f32),
            jax.ShapeDtypeStruct((16, W), f32),
        ),
        in_specs=[vmem] * 3 + [any_],
        out_specs=[hbm] * 3,
        scratch_shapes=[
            [pltpu.VMEM((rows // PARTS, T), f32)] * PARTS,
            [pltpu.VMEM((rows // PARTS, T), f32)] * PARTS,
            dma((2, PARTS)),
            dma((TT,)),
        ],
        compiler_params=pltpu.CompilerParams(vmem_limit_bytes=VMEM_LIMIT),
    )(star, change, deep, so)
    return unflattened(eo, K), unflattened(no, K), so


def solution(mesh):
    NB, NS = mesh.shape["blk"], mesh.shape["sub"]
    both = ("blk", "sub")
    return jax.shard_map(
        functools.partial(body, NB, NS),
        mesh=mesh,
        in_specs=(P(both, None, None), P(both, None, None), P(both, None), P(both), P(), P("blk", "sub")),
        out_specs=(P(both, None, None), P(both, None, None), P("blk", "sub")),
        check_vma=False,
    )
```
